32 devices in a mesh: band: 2 (over y), mesh: 16 (over z, x, core).
Axes of the slice: x: 2, y: 2, z: 4, core: 2. Of those that a mesh axis runs over, the one named last changes fastest.
Arguments:
- psi: bfloat16 [16, 1536, 1536], P('mesh', 'band'), may hold values from -6 to 6
- ritz: bfloat16 [1536, 1536], replicated, may hold values from -0.15625 to 0.15625
- cell_ham: bfloat16 [16, 4, 512, 512], P('mesh'), may hold values from -0.25 to 0.25
- cell_nodes: int32 [16, 4, 512], P('mesh'), may hold values from 0 to 1535, as said below
- face_nodes: int32 [16, 4, 256], P('mesh'), may hold values from 0 to 1535, as said below
Outputs:
- filtered: bfloat16 [16, 1536, 1536], P('mesh', None, 'band')
The draws below stay inside these ranges and needn't reach their ends.
Inputs may be any that keep to these rules, and one draw needn't show every extreme that they name: `cell_nodes`: each row of 512 entries names distinct local nodes, and every local node lies in some cell of its partition. `face_nodes`: the 1024 entries of one partition name distinct local nodes.
All inputs are finite; a program needn't handle non-finite values.
Results may differ from the reference program's by a relative error of at most 0.0058.
Values may be sent and summed in bfloat16 or wider, within the bound.
A program may use at most 64 MiB of HBM per device.

```python
import jax
import jax.numpy as jnp
from jax import lax

BANDS = 1536
NODES_CELL = 512
CELLS = 4
GRID_W = 4
NLOC = 1536
SHARED = 256
PARTS_SIZE = 16


def draw_cell_nodes(key, part):
    part_keys = jax.random.split(key, PARTS_SIZE)
    orderings = jax.vmap(lambda sub: jax.random.permutation(sub, NLOC))(part_keys)
    starts = jnp.arange(CELLS) * (NLOC - NODES_CELL) // (CELLS - 1)
    positions = starts[:, None] + jnp.arange(NODES_CELL)[None, :]
    return orderings[:, positions].astype(jnp.int32)


def draw_face_nodes(key, part):
    base_key = jax.random.fold_in(key, 7)
    part_keys = jax.random.split(base_key, PARTS_SIZE)

    def one_part(sub):
        ordering = jax.random.permutation(sub, NLOC)
        pick_at = jax.random.randint(jax.random.fold_in(sub, 3), (), 0, 4 * SHARED)
        positions = jnp.arange(NLOC)
        swapped = jnp.where(positions == pick_at, NLOC - 1, jnp.where(ordering == NLOC - 1, ordering[pick_at], ordering))
        return swapped[:4 * SHARED].reshape(4, SHARED)
    return jax.vmap(one_part)(part_keys).astype(jnp.int32)


def steps_of(rng, shape, cuts, low, top_value):
    factor_of = 1.0
    for dim, shards_of in cuts:
        heights = jax.random.uniform(jax.random.fold_in(jax.random.fold_in(rng, 6), dim), (shards_of,), jnp.float32, low / len(cuts), top_value / len(cuts))
        factor_of = factor_of * jnp.repeat(jnp.exp(heights), shape[dim] // shards_of).reshape((-1,) + (1,) * (len(shape) - 1 - dim))
    return factor_of


def centred(rng, dims, deviation, most, cuts=(), kind=jnp.bfloat16):
    result = deviation * jax.random.normal(rng, dims, jnp.float32)
    if cuts:
        result = result * steps_of(rng, dims, cuts, -0.22, 0.18)
    return jnp.clip(result, -most, most).astype(kind)


def setup_inputs(seed: int = 0) -> dict:
    key_list = jax.random.split(jax.random.key(seed), 6)
    return {
        "psi": centred(key_list[0], (PARTS_SIZE, NLOC, BANDS), 1.0, 6.0, ((0, 16), (1, 2))),
        "ritz": centred(key_list[1], (BANDS, BANDS), BANDS ** -0.5, 0.15625),
        "cell_ham": centred(key_list[2], (PARTS_SIZE, CELLS, NODES_CELL, NODES_CELL), NODES_CELL ** -0.5, 0.25, ((0, 16),)),
        "cell_nodes": draw_cell_nodes(jax.random.fold_in(key_list[5], 71), 0),
        "face_nodes": draw_face_nodes(jax.random.fold_in(key_list[5], 71), 0),
    }


def cell_products(vectors, cell_ham, cell_nodes):
    def one_part(items):
        part_vec, part_ham, part_nodes = items
        picked = part_vec[part_nodes].astype(jnp.float32)
        products = jnp.einsum("cij,cjb->cib", part_ham.astype(jnp.float32), picked)
        summed = jnp.zeros((NLOC, BANDS), jnp.float32)
        return summed.at[part_nodes.reshape(-1)].add(products.reshape(-1, BANDS))
    return lax.map(one_part, (vectors, cell_ham, cell_nodes))


def assemble(summed, face_nodes):
    rounded = lax.optimization_barrier(summed.astype(jnp.bfloat16)).astype(jnp.float32)
    flat_faces = face_nodes.reshape(PARTS_SIZE, 4 * SHARED)
    blocks = jax.vmap(lambda part_vals, rows: part_vals[rows])(rounded, flat_faces)
    blocks = blocks.reshape(PARTS_SIZE, 4, SHARED, BANDS)
    from_left = jnp.roll(blocks[:, 1], 1, axis=0)
    from_right = jnp.roll(blocks[:, 0], -1, axis=0)
    from_below = jnp.roll(blocks[:, 3], GRID_W, axis=0)
    from_above = jnp.roll(blocks[:, 2], -GRID_W, axis=0)
    arrived = jnp.stack([from_left, from_right, from_below, from_above], axis=1).reshape(PARTS_SIZE, 4 * SHARED, BANDS)
    return jax.vmap(lambda part_sum, rows, extra: part_sum.at[rows].add(extra))(summed, flat_faces, arrived)


def operator(vectors, cell_ham, cell_nodes, face_nodes):
    return assemble(cell_products(vectors, cell_ham, cell_nodes), face_nodes)


def reference(psi, ritz, cell_ham, cell_nodes, face_nodes):
    rotated = jnp.dot(psi.reshape(PARTS_SIZE * NLOC, BANDS), ritz, preferred_element_type=jnp.float32)
    rotated = rotated.astype(jnp.bfloat16).reshape(PARTS_SIZE, NLOC, BANDS)
    applied = operator(rotated, cell_ham, cell_nodes, face_nodes)
    first = ((applied - 0.25 * rotated.astype(jnp.float32)) / 2.0).astype(jnp.bfloat16)
    applied_next = operator(first, cell_ham, cell_nodes, face_nodes)
    filtered = 2.0 * (applied_next - 0.25 * first.astype(jnp.float32)) / 2.0 - rotated.astype(jnp.float32)
    return filtered.astype(jnp.bfloat16)
```

```python
import functools
import math

import jax
import jax.numpy as jnp
from jax import lax
from jax.experimental import pallas as pl
from jax.experimental.pallas import tpu as pltpu
from jax.sharding import PartitionSpec as P

GRID_W = 4
MESH = pl.DeviceIdType.MESH
BF16 = jnp.bfloat16
F32 = jnp.float32


def dot(a, b):
    return jnp.dot(a, b, preferred_element_type=F32)


def hot(condition):
    return jnp.where(condition, 1.0, 0.0).astype(BF16)


def kernel(bands, parts, psi, ritz, ham, cell_row, cell_col, node_row, node_col, out,
           turned, arrived, rotated, onehot, products, dense, summed, first, leaving, landing,
           row_send, row_recv, face_send, face_recv):
    me_b = lax.axis_index("band")
    me_p = lax.axis_index("mesh")
    chunks, nloc, width = arrived.shape
    rows = psi.shape[0]
    group = ritz.shape[1] // bands
    shared = landing.shape[3]
    face_rows = 4 * shared
    cells, size = ham.shape[0], ham.shape[1]
    tile = math.gcd(face_rows, nloc)

    routes = ((3, 2, GRID_W), (2, 3, -GRID_W), (1, 0, 1), (0, 1, -1))

    def part(offset):
        return lax.rem(me_p + offset + parts, parts)

    def partner(offset):
        return lax.rem(me_b + offset, bands)

    barrier = pltpu.get_barrier_semaphore()
    for offset in range(1, bands):
        pl.semaphore_signal(barrier, inc=1, device_id=(partner(offset), me_p), device_id_type=MESH)
    for _, _, offset in routes:
        pl.semaphore_signal(barrier, inc=1, device_id=(me_b, part(offset)), device_id_type=MESH)
    pl.semaphore_wait(barrier, bands + 3)

    def own_rows(k, owner):
        return arrived.at[k, pl.ds(pl.multiple_of(owner * rows, rows), rows), :]

    def row_copy(k, offset):
        return pltpu.make_async_remote_copy(
            src_ref=turned.at[offset - 1, k],
            dst_ref=own_rows(k, me_b),
            send_sem=row_send.at[offset - 1, k],
            recv_sem=row_recv.at[offset - 1, k],
            device_id=(partner(offset), me_p),
            device_id_type=MESH,
        )

    def ritz_columns(owner, k):
        return ritz[:, pl.ds(pl.multiple_of(owner * group + k * width, 128), width)]

    for offset in range(1, bands):
        @pl.loop(0, chunks)
        def _(k):
            turned[offset - 1, k] = dot(psi[...], ritz_columns(partner(offset), k)).astype(BF16)
            row_copy(k, offset).start()

    @pl.loop(0, chunks)
    def _(k):
        own_rows(k, me_b)[...] = dot(psi[...], ritz_columns(me_b, k)).astype(BF16)

    total = cells * size
    step = 256

    @pl.loop(0, nloc // step)
    def _(r):
        at = pl.multiple_of(r * step, step)
        numbers = lax.broadcasted_iota(jnp.int32, (step, total), 0) + at
        onehot[pl.ds(at, step), :] = hot(numbers == cell_row[...])

    @pl.loop(0, nloc // step)
    def _(c):
        at = pl.multiple_of(c * step, step)
        for cell in range(cells):
            numbers = lax.broadcasted_iota(jnp.int32, (size, step), 1) + at
            picked = hot(numbers == cell_col[cell * size:(cell + 1) * size, :])
            products[cell * size:(cell + 1) * size, :] = dot(ham[cell], picked).astype(BF16)
        for r in range(0, nloc, tile):
            dense[r:r + tile, pl.ds(at, step)] = dot(onehot[r:r + tile, :], products[...]).astype(BF16)

    @pl.loop(0, nloc // step)
    def _(r):
        at = pl.multiple_of(r * step, step)
        numbers = lax.broadcasted_iota(jnp.int32, (step, nloc), 0) + at
        onehot[pl.ds(at, step), :nloc] = hot(numbers == node_row[...])

    def face_copy(turn, k, route):
        block, slot, offset = route
        return pltpu.make_async_remote_copy(
            src_ref=leaving.at[turn, k, block],
            dst_ref=landing.at[turn, k, slot],
            send_sem=face_send.at[turn, k, slot],
            recv_sem=face_recv.at[turn, k, slot],
            device_id=(me_b, part(offset)),
            device_id_type=MESH,
        )

    def operate(turn, k, vectors):
        for half in (1, 0):
            for at in range(half * 2 * shared, (half + 1) * 2 * shared, tile):
                part_sum = dot(dense[at:at + tile, :], vectors[k])
                summed[k, at:at + tile, :] = part_sum
                rounded = part_sum.astype(BF16)
                for block in range(at // shared, max(at // shared + 1, (at + tile) // shared)):
                    low = max(at, block * shared)
                    high = min(at + tile, (block + 1) * shared)
                    leaving[turn, k, block, low - block * shared:high - block * shared, :] = rounded[low - at:high - at]
            for route in routes:
                if route[0] // 2 == half:
                    face_copy(turn, k, route).start()
        for at in range(face_rows, nloc, tile):
            summed[k, at:at + tile, :] = dot(dense[at:at + tile, :], vectors[k])

    @pl.loop(0, chunks)
    def _(k):
        for offset in range(1, bands):
            row_copy(k, offset).wait()
        for r in range(0, nloc, tile):
            rotated[k, r:r + tile, :] = dot(onehot[r:r + tile, :nloc], arrived[k]).astype(BF16)
        operate(0, k, rotated)

    def assembled(turn, k):
        for route in routes:
            face_copy(turn, k, route).wait()
        for slot in range(4):
            at = slice(slot * shared, (slot + 1) * shared)
            summed[k, at, :] = summed[k, at, :] + landing[turn, k, slot].astype(F32)

    @pl.loop(0, chunks)
    def _(k):
        assembled(0, k)
        first[k] = ((summed[k] - 0.25 * rotated[k].astype(F32)) / 2.0).astype(BF16)
        operate(1, k, first)

    @pl.loop(0, nloc // step)
    def _(r):
        at = pl.multiple_of(r * step, step)
        numbers = lax.broadcasted_iota(jnp.int32, (step, nloc), 1)
        onehot[pl.ds(at, step), :nloc] = hot(numbers == node_col[pl.ds(at, step), :])

    @pl.loop(0, chunks)
    def _(k):
        assembled(1, k)
        value = 2.0 * (summed[k] - 0.25 * first[k].astype(F32)) / 2.0 - rotated[k].astype(F32)
        arrived[k] = value.astype(BF16)
        columns = pl.ds(pl.multiple_of(k * width, 128), width)
        for r in range(0, nloc, tile):
            out[r:r + tile, columns] = dot(onehot[r:r + tile, :nloc], arrived[k]).astype(BF16)


def local(bands, parts, psi, ritz, cell_ham, cell_nodes, face_nodes):
    rows = psi.shape[1]
    nloc = rows * bands
    group = ritz.shape[1] // bands
    cells, size = cell_ham.shape[1], cell_ham.shape[2]
    shared = face_nodes.shape[2]
    faces = face_nodes.reshape(-1)
    numbers = jnp.arange(nloc, dtype=jnp.int32)
    match = faces[:, None] == numbers[None, :]
    order = jnp.arange(1, faces.shape[0] + 1, dtype=jnp.int32)
    face_at = jnp.sum(jnp.where(match, order[:, None], 0), axis=0)
    inner = face_at == 0
    before = jnp.sum(jnp.where((numbers[:, None] < numbers[None, :]) & inner[:, None], 1, 0), axis=0)
    place = jnp.where(inner, faces.shape[0] + before, face_at - 1).astype(jnp.int32)
    nodes = cell_nodes.reshape(-1)
    cell_place = jnp.sum(jnp.where(nodes[:, None] == numbers[None, :], place[None, :], 0), axis=1).astype(jnp.int32)

    width = 256 if group % 256 == 0 else 128
    chunks = group // width
    vmem = pl.BlockSpec(memory_space=pltpu.VMEM)
    out = pl.pallas_call(
        functools.partial(kernel, bands, parts),
        out_shape=jax.ShapeDtypeStruct((nloc, group), BF16),
        in_specs=[vmem] * 7,
        out_specs=vmem,
        scratch_shapes=[
            pltpu.VMEM((bands - 1, chunks, rows, width), BF16),
            pltpu.VMEM((chunks, nloc, width), BF16),
            pltpu.VMEM((chunks, nloc, width), BF16),
            pltpu.VMEM((nloc, max(cells * size, nloc)), BF16),
            pltpu.VMEM((cells * size, 256), BF16),
            pltpu.VMEM((nloc, nloc), BF16),
            pltpu.VMEM((chunks, nloc, width), F32),
            pltpu.VMEM((chunks, nloc, width), BF16),
            pltpu.VMEM((2, chunks, 4, shared, width), BF16),
            pltpu.VMEM((2, chunks, 4, shared, width), BF16),
            pltpu.SemaphoreType.DMA((bands - 1, chunks)),
            pltpu.SemaphoreType.DMA((bands - 1, chunks)),
            pltpu.SemaphoreType.DMA((2, chunks, 4)),
            pltpu.SemaphoreType.DMA((2, chunks, 4)),
        ],
        compiler_params=pltpu.CompilerParams(
            collective_id=0, has_side_effects=True, vmem_limit_bytes=62 * 1024 * 1024
        ),
    )(psi[0], ritz, cell_ham[0], cell_place[None, :], cell_place[:, None], place[None, :], place[:, None])
    return out[None]


def solution(mesh):
    return jax.shard_map(
        functools.partial(local, mesh.shape["band"], mesh.shape["mesh"]),
        mesh=mesh,
        in_specs=(
            P("mesh", "band", None),
            P(),
            P("mesh", None, None, None),
            P("mesh", None, None),
            P("mesh", None, None),
        ),
        out_specs=P("mesh", None, "band"),
        check_vma=False,
    )
```

```python
import functools
import math

import jax
import jax.numpy as jnp
from jax import lax
from jax.experimental import pallas as pl
from jax.experimental.pallas import tpu as pltpu
from jax.sharding import PartitionSpec as P

GRID_W = 4
MESH = pl.DeviceIdType.MESH
BF16 = jnp.bfloat16
F32 = jnp.float32


def dot(a, b):
    return jnp.dot(a, b, preferred_element_type=F32)


def hot(condition):
    return jnp.where(condition, 1.0, 0.0).astype(BF16)


def upright(row):
    return jnp.broadcast_to(row, (128, row.shape[1])).T


def across(column, width):
    return jnp.concatenate([column] * (width // 128), axis=1)


def kernel(bands, parts, psi_hbm, ritz_hbm, ham_hbm, cell_nodes, face_nodes, out,
           psi, ritz, ham, turned, arrived, rotated, cell_hot, node_hot, picked, dense, summed, first, leaving, landing,
           columns, finished, load, store, row_send, row_recv, face_send, face_recv):
    me_b = lax.axis_index("band")
    me_p = lax.axis_index("mesh")
    chunks, nloc, width = arrived.shape
    rows = psi.shape[0]
    group = ritz.shape[2]
    shared = landing.shape[3]
    face_rows = 4 * shared
    cells, size = ham.shape[0], ham.shape[1]
    total = cells * size
    tile = math.gcd(2 * shared, nloc)
    step = 256

    routes = ((3, 2, GRID_W), (2, 3, -GRID_W), (1, 0, 1), (0, 1, -1))

    def part(offset):
        return lax.rem(me_p + offset + parts, parts)

    def partner(offset):
        return lax.rem(me_b + offset, bands)

    def ritz_load(offset):
        at = pl.multiple_of(partner(offset) * group, 128)
        return pltpu.make_async_copy(ritz_hbm.at[:, pl.ds(at, group)], ritz.at[offset], load.at[2 + offset])

    psi_load = pltpu.make_async_copy(psi_hbm, psi, load.at[0])
    ham_load = pltpu.make_async_copy(ham_hbm, ham, load.at[1])
    psi_load.start()
    for offset in range(1, bands):
        ritz_load(offset).start()
    ritz_load(0).start()
    ham_load.start()

    barrier = pltpu.get_barrier_semaphore()
    for offset in range(1, bands):
        pl.semaphore_signal(barrier, inc=1, device_id=(partner(offset), me_p), device_id_type=MESH)
    for _, _, offset in routes:
        pl.semaphore_signal(barrier, inc=1, device_id=(me_b, part(offset)), device_id_type=MESH)
    pl.semaphore_wait(barrier, bands + 3)

    def own_rows(k, owner):
        return arrived.at[k, pl.ds(pl.multiple_of(owner * rows, rows), rows), :]

    def row_copy(k, offset):
        return pltpu.make_async_remote_copy(
            src_ref=turned.at[offset - 1, k],
            dst_ref=own_rows(k, me_b),
            send_sem=row_send.at[offset - 1, k],
            recv_sem=row_recv.at[offset - 1, k],
            device_id=(partner(offset), me_p),
            device_id_type=MESH,
        )

    def chunk(k):
        return pl.ds(pl.multiple_of(k * width, 128), width)

    psi_load.wait()
    for offset in range(1, bands):
        ritz_load(offset).wait()

    @pl.loop(0, chunks)
    def _(k):
        for offset in range(1, bands):
            turned[offset - 1, k] = dot(psi[...], ritz[offset, :, chunk(k)]).astype(BF16)
            row_copy(k, offset).start()

    for face in range(4):
        columns[face * shared:(face + 1) * shared, :] = upright(face_nodes[face:face + 1, :])
    lanes = lax.broadcasted_iota(jnp.int32, (1, nloc), 1)

    def find_face(block, found):
        at = pl.multiple_of(block * step, step)
        order = lax.broadcasted_iota(jnp.int32, (step, nloc), 0) + (at + 1)
        numbers = lax.broadcasted_iota(jnp.int32, (step, nloc), 1)
        match = across(columns[pl.ds(at, step), :], nloc) == numbers
        return found + jnp.sum(jnp.where(match, order, 0), axis=0, keepdims=True)

    found = lax.fori_loop(0, face_rows // step, find_face, jnp.zeros((1, nloc), jnp.int32))
    inner = jnp.where(found == 0, 1, 0)
    before = jnp.broadcast_to(inner, (8, nloc))
    eight = lax.broadcasted_iota(jnp.int32, (8, nloc), 1)
    shift = 1
    while shift < nloc:
        before = before + jnp.where(eight >= shift, pltpu.roll(before, shift, 1), 0)
        shift *= 2
    place = jnp.where(found == 0, before[:1, :] + (face_rows - 1), found - 1)

    @pl.loop(0, nloc // step)
    def _(r):
        at = pl.multiple_of(r * step, step)
        numbers = lax.broadcasted_iota(jnp.int32, (step, nloc), 0) + at
        node_hot[pl.ds(at, step), :] = hot(numbers == place)

    columns[:nloc, :] = upright(place)
    listed = jnp.concatenate([cell_nodes[cell:cell + 1, :] for cell in range(cells)], axis=1)

    def find_place(block, places):
        at = pl.multiple_of(block * step, step)
        numbers = lax.broadcasted_iota(jnp.int32, (step, total), 0) + at
        values = across(columns[pl.ds(at, step), :], total)
        return places + jnp.sum(jnp.where(numbers == listed, values, 0), axis=0, keepdims=True)

    cell_place = lax.fori_loop(0, nloc // step, find_place, jnp.zeros((1, total), jnp.int32))
    columns[nloc:, :] = upright(cell_place)

    @pl.loop(0, total // step)
    def _(r):
        at = pl.multiple_of(r * step, step)
        numbers = lax.broadcasted_iota(jnp.int32, (step, nloc), 1)
        cell_hot[pl.ds(at, step), :nloc] = hot(numbers == across(columns[pl.ds(nloc + at, step), :], nloc))

    ritz_load(0).wait()

    @pl.loop(0, chunks)
    def _(k):
        own_rows(k, me_b)[...] = dot(psi[...], ritz[0, :, chunk(k)]).astype(BF16)

    ham_load.wait()

    def build(low, high):
        for at in range(low, high, tile):
            numbers = lax.broadcasted_iota(jnp.int32, (tile, size), 0) + at
            for cell in range(cells):
                span = slice(cell * size, (cell + 1) * size)
                picked[:, span] = dot(hot(numbers == cell_place[:, span]), ham[cell]).astype(BF16)

            @pl.loop(0, nloc // step)
            def _(c):
                to = pl.multiple_of(c * step, step)
                dense[at:at + tile, pl.ds(to, step)] = dot(picked[...], cell_hot[:, pl.ds(to, step)]).astype(BF16)

    def face_copy(turn, k, route):
        block, slot, offset = route
        return pltpu.make_async_remote_copy(
            src_ref=leaving.at[turn, k, block],
            dst_ref=landing.at[turn, k, slot],
            send_sem=face_send.at[turn, k, slot],
            recv_sem=face_recv.at[turn, k, slot],
            device_id=(me_b, part(offset)),
            device_id_type=MESH,
        )

    def operate_faces(turn, k, vectors, half):
        for at in range(half * 2 * shared, (half + 1) * 2 * shared, tile):
            part_sum = dot(dense[at:at + tile, :], vectors[k])
            summed[k, at:at + tile, :] = part_sum
            rounded = part_sum.astype(BF16)
            for block in range(4):
                low = max(at, block * shared)
                high = min(at + tile, (block + 1) * shared)
                if low < high:
                    leaving[turn, k, block, low - block * shared:high - block * shared, :] = rounded[low - at:high - at]
        for route in routes:
            if route[0] // 2 == half:
                face_copy(turn, k, route).start()

    def operate_inner(k, vectors):
        for at in range(face_rows, nloc, tile):
            summed[k, at:at + tile, :] = dot(dense[at:at + tile, :], vectors[k])

    def receive(k):
        for offset in range(1, bands):
            row_copy(k, offset).wait()

        @pl.loop(0, nloc // tile)
        def _(r):
            at = pl.ds(pl.multiple_of(r * tile, tile), tile)
            rotated[k, at, :] = dot(node_hot[at, :], arrived[k]).astype(BF16)

    build(2 * shared, face_rows)
    receive(0)
    operate_faces(0, 0, rotated, 1)
    build(0, 2 * shared)
    operate_faces(0, 0, rotated, 0)

    @pl.loop(1, chunks)
    def _(k):
        receive(k)
        operate_faces(0, k, rotated, 1)
        operate_faces(0, k, rotated, 0)

    build(face_rows, nloc)

    def assembled(turn, k):
        for route in routes:
            face_copy(turn, k, route).wait()
        for slot in range(4):
            at = slice(slot * shared, (slot + 1) * shared)
            summed[k, at, :] = summed[k, at, :] + landing[turn, k, slot].astype(F32)

    @pl.loop(0, chunks)
    def _(k):
        operate_inner(k, rotated)
        assembled(0, k)
        first[k] = ((summed[k] - 0.25 * rotated[k].astype(F32)) / 2.0).astype(BF16)
        operate_faces(1, k, first, 1)
        operate_faces(1, k, first, 0)
        operate_inner(k, first)

    @pl.loop(0, nloc // step)
    def _(r):
        at = pl.multiple_of(r * step, step)
        numbers = lax.broadcasted_iota(jnp.int32, (step, nloc), 1)
        node_hot[pl.ds(at, step), :] = hot(numbers == across(columns[pl.ds(at, step), :], nloc))

    def put(k):
        return pltpu.make_async_copy(finished.at[k], out.at[:, chunk(k)], store.at[k])

    @pl.loop(0, chunks)
    def _(k):
        assembled(1, k)
        value = 2.0 * (summed[k] - 0.25 * first[k].astype(F32)) / 2.0 - rotated[k].astype(F32)
        arrived[k] = value.astype(BF16)

        @pl.loop(0, nloc // tile)
        def _(r):
            at = pl.ds(pl.multiple_of(r * tile, tile), tile)
            finished[k, at, :] = dot(node_hot[at, :], arrived[k]).astype(BF16)

        put(k).start()

    @pl.loop(0, chunks)
    def _(k):
        put(k).wait()


def local(bands, parts, psi, ritz, cell_ham, cell_nodes, face_nodes):
    rows = psi.shape[1]
    nloc = rows * bands
    group = ritz.shape[1] // bands
    cells, size = cell_ham.shape[1], cell_ham.shape[2]
    shared = face_nodes.shape[2]
    width = 256 if group % 256 == 0 else 128
    chunks = group // width
    tile = math.gcd(2 * shared, nloc)
    anywhere = pl.BlockSpec(memory_space=pl.ANY)
    vmem = pl.BlockSpec(memory_space=pltpu.VMEM)
    out = pl.pallas_call(
        functools.partial(kernel, bands, parts),
        out_shape=jax.ShapeDtypeStruct((nloc, group), BF16),
        in_specs=[anywhere] * 3 + [vmem] * 2,
        out_specs=anywhere,
        scratch_shapes=[
            pltpu.VMEM((rows, ritz.shape[0]), BF16),
            pltpu.VMEM((bands, ritz.shape[0], group), BF16),
            pltpu.VMEM((cells, size, size), BF16),
            pltpu.VMEM((bands - 1, chunks, rows, width), BF16),
            pltpu.VMEM((chunks, nloc, width), BF16),
            pltpu.VMEM((chunks, nloc, width), BF16),
            pltpu.VMEM((cells * size, nloc), BF16),
            pltpu.VMEM((nloc, nloc), BF16),
            pltpu.VMEM((tile, cells * size), BF16),
            pltpu.VMEM((nloc, nloc), BF16),
            pltpu.VMEM((chunks, nloc, width), F32),
            pltpu.VMEM((chunks, nloc, width), BF16),
            pltpu.VMEM((2, chunks, 4, shared, width), BF16),
            pltpu.VMEM((2, chunks, 4, shared, width), BF16),
            pltpu.VMEM((nloc + cells * size, 128), jnp.int32),
            pltpu.VMEM((chunks, nloc, width), BF16),
            pltpu.SemaphoreType.DMA((2 + bands,)),
            pltpu.SemaphoreType.DMA((chunks,)),
            pltpu.SemaphoreType.DMA((bands - 1, chunks)),
            pltpu.SemaphoreType.DMA((bands - 1, chunks)),
            pltpu.SemaphoreType.DMA((2, chunks, 4)),
            pltpu.SemaphoreType.DMA((2, chunks, 4)),
        ],
        compiler_params=pltpu.CompilerParams(
            collective_id=0, has_side_effects=True, vmem_limit_bytes=62 * 1024 * 1024
        ),
    )(psi[0], ritz, cell_ham[0], cell_nodes[0], face_nodes[0])
    return out[None]


def solution(mesh):
    return jax.shard_map(
        functools.partial(local, mesh.shape["band"], mesh.shape["mesh"]),
        mesh=mesh,
        in_specs=(
            P("mesh", "band", None),
            P(),
            P("mesh", None, None, None),
            P("mesh", None, None),
            P("mesh", None, None),
        ),
        out_specs=P("mesh", None, "band"),
        check_vma=False,
    )
```

```python
import functools
import math

import jax
import jax.numpy as jnp
from jax import lax
from jax.experimental import pallas as pl
from jax.experimental.pallas import tpu as pltpu
from jax.sharding import PartitionSpec as P

GRID_W = 4
MESH = pl.DeviceIdType.MESH
BF16 = jnp.bfloat16
F32 = jnp.float32


def dot(a, b):
    return jnp.dot(a, b, preferred_element_type=F32)


def hot(condition):
    return jnp.where(condition, 1.0, 0.0).astype(BF16)


def upright(row):
    return jnp.broadcast_to(row, (128, row.shape[1])).T


def across(column, width):
    return jnp.concatenate([column] * (width // 128), axis=1)


def kernel(bands, parts, psi_hbm, ritz_hbm, ham_hbm, cell_nodes, face_nodes, out,
           psi, ritz, ham, turned, arrived, rotated, cell_hot, node_hot, picked, dense, summed, first, leaving, landing,
           columns, finished, load, store, row_send, row_recv, face_send, face_recv):
    me_b = lax.axis_index("band")
    me_p = lax.axis_index("mesh")
    chunks, nloc, width = arrived.shape
    rows = psi.shape[0]
    group = ritz.shape[2]
    shared = landing.shape[3]
    face_rows = 4 * shared
    cells, size = ham.shape[0], ham.shape[1]
    total = cells * size
    tile = math.gcd(2 * shared, nloc)
    step = 256

    routes = ((3, 2, GRID_W), (2, 3, -GRID_W), (1, 0, 1), (0, 1, -1))

    def part(offset):
        return lax.rem(me_p + offset + parts, parts)

    def partner(offset):
        return lax.rem(me_b + offset, bands)

    def ritz_load(offset):
        at = pl.multiple_of(partner(offset) * group, 128)
        return pltpu.make_async_copy(ritz_hbm.at[:, pl.ds(at, group)], ritz.at[offset], load.at[2 + offset])

    psi_load = pltpu.make_async_copy(psi_hbm, psi, load.at[0])
    ham_load = pltpu.make_async_copy(ham_hbm, ham, load.at[1])
    psi_load.start()
    for offset in range(1, bands):
        ritz_load(offset).start()
    ritz_load(0).start()
    ham_load.start()

    barrier = pltpu.get_barrier_semaphore()
    for offset in range(1, bands):
        pl.semaphore_signal(barrier, inc=1, device_id=(partner(offset), me_p), device_id_type=MESH)
    for _, _, offset in routes:
        pl.semaphore_signal(barrier, inc=1, device_id=(me_b, part(offset)), device_id_type=MESH)

    def own_rows(k, owner):
        return arrived.at[k, pl.ds(pl.multiple_of(owner * rows, rows), rows), :]

    def row_copy(k, offset):
        return pltpu.make_async_remote_copy(
            src_ref=turned.at[offset - 1, k],
            dst_ref=own_rows(k, me_b),
            send_sem=row_send.at[offset - 1, k],
            recv_sem=row_recv.at[offset - 1, k],
            device_id=(partner(offset), me_p),
            device_id_type=MESH,
        )

    def chunk(k):
        return pl.ds(pl.multiple_of(k * width, 128), width)

    for face in range(4):
        columns[face * shared:(face + 1) * shared, :] = upright(face_nodes[face:face + 1, :])
    lanes = lax.broadcasted_iota(jnp.int32, (1, nloc), 1)

    def find_face(block, found):
        at = pl.multiple_of(block * step, step)
        order = lax.broadcasted_iota(jnp.int32, (step, nloc), 0) + (at + 1)
        numbers = lax.broadcasted_iota(jnp.int32, (step, nloc), 1)
        match = across(columns[pl.ds(at, step), :], nloc) == numbers
        return found + jnp.sum(jnp.where(match, order, 0), axis=0, keepdims=True)

    found = lax.fori_loop(0, face_rows // step, find_face, jnp.zeros((1, nloc), jnp.int32))
    inner = jnp.where(found == 0, 1, 0)
    before = jnp.broadcast_to(inner, (8, nloc))
    eight = lax.broadcasted_iota(jnp.int32, (8, nloc), 1)
    shift = 1
    while shift < nloc:
        before = before + jnp.where(eight >= shift, pltpu.roll(before, shift, 1), 0)
        shift *= 2
    place = jnp.where(found == 0, before[:1, :] + (face_rows - 1), found - 1)

    @pl.loop(0, nloc // step)
    def _(r):
        at = pl.multiple_of(r * step, step)
        numbers = lax.broadcasted_iota(jnp.int32, (step, nloc), 0) + at
        node_hot[pl.ds(at, step), :] = hot(numbers == place)

    columns[:nloc, :] = upright(place)
    listed = jnp.concatenate([cell_nodes[cell:cell + 1, :] for cell in range(cells)], axis=1)

    def find_place(block, places):
        at = pl.multiple_of(block * step, step)
        numbers = lax.broadcasted_iota(jnp.int32, (step, total), 0) + at
        values = across(columns[pl.ds(at, step), :], total)
        return places + jnp.sum(jnp.where(numbers == listed, values, 0), axis=0, keepdims=True)

    cell_place = lax.fori_loop(0, nloc // step, find_place, jnp.zeros((1, total), jnp.int32))
    columns[nloc:, :] = upright(cell_place)

    @pl.loop(0, total // step)
    def _(r):
        at = pl.multiple_of(r * step, step)
        numbers = lax.broadcasted_iota(jnp.int32, (step, nloc), 1)
        cell_hot[pl.ds(at, step), :nloc] = hot(numbers == across(columns[pl.ds(nloc + at, step), :], nloc))

    def turn(k):
        for offset in range(1, bands):
            turned[offset - 1, k] = dot(psi[...], ritz[offset, :, chunk(k)]).astype(BF16)
            row_copy(k, offset).start()

    def keep(k):
        own_rows(k, me_b)[...] = dot(psi[...], ritz[0, :, chunk(k)]).astype(BF16)

    psi_load.wait()
    for offset in range(1, bands):
        ritz_load(offset).wait()
    pl.semaphore_wait(barrier, bands + 3)
    turn(0)
    ritz_load(0).wait()
    keep(0)
    ham_load.wait()

    def build(low, high):
        for at in range(low, high, tile):
            numbers = lax.broadcasted_iota(jnp.int32, (tile, size), 0) + at
            for cell in range(cells):
                span = slice(cell * size, (cell + 1) * size)
                picked[:, span] = dot(hot(numbers == cell_place[:, span]), ham[cell]).astype(BF16)

            @pl.loop(0, nloc // step)
            def _(c):
                to = pl.multiple_of(c * step, step)
                dense[at:at + tile, pl.ds(to, step)] = dot(picked[...], cell_hot[:, pl.ds(to, step)]).astype(BF16)

    def face_copy(turn, k, route):
        block, slot, offset = route
        return pltpu.make_async_remote_copy(
            src_ref=leaving.at[turn, k, block],
            dst_ref=landing.at[turn, k, slot],
            send_sem=face_send.at[turn, k, slot],
            recv_sem=face_recv.at[turn, k, slot],
            device_id=(me_b, part(offset)),
            device_id_type=MESH,
        )

    def operate_faces(turn, k, vectors, half):
        for at in range(half * 2 * shared, (half + 1) * 2 * shared, tile):
            part_sum = dot(dense[at:at + tile, :], vectors[k])
            summed[k, at:at + tile, :] = part_sum
            rounded = part_sum.astype(BF16)
            for block in range(4):
                low = max(at, block * shared)
                high = min(at + tile, (block + 1) * shared)
                if low < high:
                    leaving[turn, k, block, low - block * shared:high - block * shared, :] = rounded[low - at:high - at]
        for late in (False, True):
            for route in routes:
                if route[0] // 2 == half:
                    target = me_p + route[2]
                    wraps = jnp.logical_or(target < 0, target >= parts)

                    @pl.when(wraps if late else jnp.logical_not(wraps))
                    def _(route=route):
                        face_copy(turn, k, route).start()

    def operate_inner(k, vectors):
        for at in range(face_rows, nloc, tile):
            summed[k, at:at + tile, :] = dot(dense[at:at + tile, :], vectors[k])

    def receive(k):
        for offset in range(1, bands):
            row_copy(k, offset).wait()

        @pl.loop(0, nloc // tile)
        def _(r):
            at = pl.ds(pl.multiple_of(r * tile, tile), tile)
            rotated[k, at, :] = dot(node_hot[at, :], arrived[k]).astype(BF16)

    def assembled(turn, k):
        for route in routes:
            face_copy(turn, k, route).wait()
        for slot in range(4):
            at = slice(slot * shared, (slot + 1) * shared)
            summed[k, at, :] = summed[k, at, :] + landing[turn, k, slot].astype(F32)

    def advance(k):
        operate_inner(k, rotated)
        assembled(0, k)
        first[k] = ((summed[k] - 0.25 * rotated[k].astype(F32)) / 2.0).astype(BF16)
        operate_faces(1, k, first, 1)
        operate_faces(1, k, first, 0)

    build(2 * shared, face_rows)

    @pl.loop(1, chunks)
    def _(k):
        turn(k)

    @pl.loop(1, chunks)
    def _(k):
        keep(k)

    receive(0)
    operate_faces(0, 0, rotated, 1)
    build(0, 2 * shared)
    operate_faces(0, 0, rotated, 0)

    @pl.loop(1, chunks)
    def _(k):
        receive(k)
        operate_faces(0, k, rotated, 1)
        operate_faces(0, k, rotated, 0)

        @pl.when(k == 1)
        def _():
            build(face_rows, nloc)

        advance(k - 1)

    if chunks == 1:
        build(face_rows, nloc)
    advance(chunks - 1)

    @pl.loop(0, nloc // step)
    def _(r):
        at = pl.multiple_of(r * step, step)
        numbers = lax.broadcasted_iota(jnp.int32, (step, nloc), 1)
        node_hot[pl.ds(at, step), :] = hot(numbers == across(columns[pl.ds(at, step), :], nloc))

    def put(k):
        return pltpu.make_async_copy(finished.at[k], out.at[:, chunk(k)], store.at[k])

    @pl.loop(0, chunks)
    def _(k):
        operate_inner(k, first)
        assembled(1, k)
        value = 2.0 * (summed[k] - 0.25 * first[k].astype(F32)) / 2.0 - rotated[k].astype(F32)
        arrived[k] = value.astype(BF16)

        @pl.loop(0, nloc // tile)
        def _(r):
            at = pl.ds(pl.multiple_of(r * tile, tile), tile)
            finished[k, at, :] = dot(node_hot[at, :], arrived[k]).astype(BF16)

        put(k).start()

    @pl.loop(0, chunks)
    def _(k):
        put(k).wait()


def copy_kernel(source, target, held, taken, given):
    pieces, rows = held.shape[0], held.shape[1]

    def take(i):
        return pltpu.make_async_copy(source.at[i * rows:(i + 1) * rows, :], held.at[i], taken.at[i])

    def give(i):
        return pltpu.make_async_copy(held.at[i], target.at[i * rows:(i + 1) * rows, :], given.at[i])

    for i in range(pieces):
        take(i).start()
    for i in range(pieces):
        take(i).wait()
        give(i).start()
    for i in range(pieces):
        give(i).wait()


def local(bands, parts, psi, ritz, cell_ham, cell_nodes, face_nodes):
    rows = psi.shape[1]
    nloc = rows * bands
    group = ritz.shape[1] // bands
    cells, size = cell_ham.shape[1], cell_ham.shape[2]
    shared = face_nodes.shape[2]
    width = 256 if group % 256 == 0 else 128
    chunks = group // width
    tile = math.gcd(2 * shared, nloc)
    anywhere = pl.BlockSpec(memory_space=pl.ANY)
    vmem = pl.BlockSpec(memory_space=pltpu.VMEM)
    out = pl.pallas_call(
        functools.partial(kernel, bands, parts),
        out_shape=jax.ShapeDtypeStruct((nloc, group), BF16),
        in_specs=[anywhere] * 3 + [vmem] * 2,
        out_specs=anywhere,
        scratch_shapes=[
            pltpu.VMEM((rows, ritz.shape[0]), BF16),
            pltpu.VMEM((bands, ritz.shape[0], group), BF16),
            pltpu.VMEM((cells, size, size), BF16),
            pltpu.VMEM((bands - 1, chunks, rows, width), BF16),
            pltpu.VMEM((chunks, nloc, width), BF16),
            pltpu.VMEM((chunks, nloc, width), BF16),
            pltpu.VMEM((cells * size, nloc), BF16),
            pltpu.VMEM((nloc, nloc), BF16),
            pltpu.VMEM((tile, cells * size), BF16),
            pltpu.VMEM((nloc, nloc), BF16),
            pltpu.VMEM((chunks, nloc, width), F32),
            pltpu.VMEM((chunks, nloc, width), BF16),
            pltpu.VMEM((2, chunks, 4, shared, width), BF16),
            pltpu.VMEM((2, chunks, 4, shared, width), BF16),
            pltpu.VMEM((nloc + cells * size, 128), jnp.int32),
            pltpu.VMEM((chunks, nloc, width), BF16),
            pltpu.SemaphoreType.DMA((2 + bands,)),
            pltpu.SemaphoreType.DMA((chunks,)),
            pltpu.SemaphoreType.DMA((bands - 1, chunks)),
            pltpu.SemaphoreType.DMA((bands - 1, chunks)),
            pltpu.SemaphoreType.DMA((2, chunks, 4)),
            pltpu.SemaphoreType.DMA((2, chunks, 4)),
        ],
        compiler_params=pltpu.CompilerParams(
            collective_id=0, has_side_effects=True, vmem_limit_bytes=62 * 1024 * 1024
        ),
    )(psi[0], ritz, cell_ham[0], cell_nodes[0], face_nodes[0])
    pieces = 6 if nloc % 48 == 0 else 1
    out = pl.pallas_call(
        copy_kernel,
        out_shape=jax.ShapeDtypeStruct((nloc, group), BF16),
        in_specs=[anywhere],
        out_specs=anywhere,
        scratch_shapes=[
            pltpu.VMEM((pieces, nloc // pieces, group), BF16),
            pltpu.SemaphoreType.DMA((pieces,)),
            pltpu.SemaphoreType.DMA((pieces,)),
        ],
    )(out)
    return out[None]


def solution(mesh):
    return jax.shard_map(
        functools.partial(local, mesh.shape["band"], mesh.shape["mesh"]),
        mesh=mesh,
        in_specs=(
            P("mesh", "band", None),
            P(),
            P("mesh", None, None, None),
            P("mesh", None, None),
            P("mesh", None, None),
        ),
        out_specs=P("mesh", None, "band"),
        check_vma=False,
    )
```
